32 devices in a mesh: dp: 4 (over y, x), expert: 8 (over z, core).
Axes of the slice: x: 2, y: 2, z: 4, core: 2. Of those that a mesh axis runs over, the one named last changes fastest.
Arguments:
- out_grad: bfloat16 [4096, 2048], P(('dp', 'expert')), may hold values from -1.1953125 to 1.1953125
- saved_hidden: bfloat16 [4096, 8, 384], P(('dp', 'expert')), may hold values from -6 to 6
- gate_weight: bfloat16 [4096, 8], P(('dp', 'expert')), may hold values from 0.19921875 to 1
- expert_ids: int32 [4096, 8], P(('dp', 'expert')), may hold values from 0 to 31, all different within a row; in each aligned block of 128 rows (0 to 127, 128 to 255, ...) at most 48 rows name the same one
- down_weight: bfloat16 [2048, 32, 384], P('dp', 'expert'), may hold values from -0.3125 to 0.3125
Outputs:
- grad_hidden: bfloat16 [4096, 8, 384], P(('dp', 'expert'))
- grad_gate: bfloat16 [4096, 8], P(('dp', 'expert'))
- grad_down: float32 [2048, 32, 384], P('dp', 'expert')
The draws below stay inside these ranges and needn't reach their ends.
Inputs may be any that keep to these rules, and one draw needn't show every extreme that they name: `expert_ids`: each token names 8 different experts. Among the tokens of one device no expert is named by more than 48 tokens, and in every draw some expert is named by exactly 48 tokens of some device.
All inputs are finite; a program needn't handle non-finite values.
Results may differ from the reference program's by a relative error of at most 0.014.
Values may be sent and summed in bfloat16 or wider, within the bound.
A program may use at most 128 MiB of HBM per device.

```python
import math
import jax
import jax.numpy as jnp
import numpy as np
from jax import lax

D = 2048
FF = 384
TOPK = 8
TOK_DEV = 128
EXPERTS = 32
TOKENS = 4096
CAP = 48
N_DP = 4
N_EXPERT = 8


def with_spikes(values, rng, source, target, parts, factor):
    owner, partner = [(jnp.arange(values.shape[dim]) // (values.shape[dim] // parts)).reshape([-1 if axis == dim else 1 for axis in range(values.ndim)]) for dim in (source, target)]
    chosen = jax.random.permutation(rng, parts)[partner]
    strong = (owner == chosen) | (owner == (partner + parts // 2) % parts)
    return jnp.where(strong, factor * values, values)


def shard_levels(stream_key, extent, split, least, top_value):
    loudness = 1.0
    for position, blocks in split:
        steps = jax.random.uniform(jax.random.fold_in(jax.random.fold_in(stream_key, 6), position), (blocks,), jnp.float32, least / len(split), top_value / len(split))
        loudness = loudness * jnp.repeat(jnp.exp(steps), extent[position] // blocks).reshape((-1,) + (1,) * (len(extent) - 1 - position))
    return loudness


def deal_out(own_key, own, number, rows, number_of, top, bound, slope):
    order = jax.random.permutation(own_key, number_of)
    heavy_load, usual = shares(number_of, rows * top, bound, slope, True), shares(number_of, rows * top, bound, slope, False)
    places = jnp.arange(number_of)

    def named(lengths, rotation):
        used = int((lengths > 0).sum())
        fixed = max(1, used // 4)
        passed = fixed + (places - fixed + rotation * (used - fixed)) % max(1, number_of - fixed)
        return jnp.zeros((number_of,), jnp.int32).at[order[jnp.where(places < fixed, places, passed)]].set(jnp.asarray(lengths, jnp.int32))

    lengths = jnp.where(number % 4 == 0, named(heavy_load, number // 4), named(usual, number - number // 4 - 1))
    mixed = jax.random.permutation(jax.random.fold_in(own, 3), number_of)
    donor, sink = mixed[0:number_of // 2 * 2:2], mixed[1:number_of // 2 * 2:2]
    room = jnp.minimum(lengths[donor] - 1, bound - lengths[sink]) // 2
    room = jnp.where((donor == order[0]) | (sink == order[0]) | (lengths[sink] == 0), 0, jnp.maximum(room, 0))
    passed = jax.random.randint(jax.random.fold_in(own, 4), (number_of // 2,), 0, 1 << 20) % (room + 1)
    lengths = lengths.at[donor].add(-passed).at[sink].add(passed)
    members = jnp.searchsorted(jnp.cumsum(lengths), jnp.arange(rows * top), side="right").astype(jnp.int32)
    table = members.reshape(top, rows).T
    table = table[jax.random.permutation(jax.random.fold_in(own, 1), rows)]
    rotation = jax.random.randint(jax.random.fold_in(own, 2), (rows, 1), 0, top)
    return jnp.take_along_axis(table, (jnp.arange(top)[None, :] + rotation) % top, axis=1)


def shares(amount, total, most, slope, full):
    weights = [(1 << 20) // math.isqrt(standing ** slope) + 1 for standing in range(1, amount + 1)]
    largest = most if full else min(most, max(-(-total // amount), total * weights[0] // sum(weights)))
    least = 1 if total - largest >= amount - 1 else 0
    counts, rest = [largest] + [least] * (amount - 1), total - largest - least * (amount - 1)
    while rest > 0:
        movable = [i for i in range(1, amount) if counts[i] < largest] or [i for i in range(1, amount) if counts[i] < most]
        pool, budget = sum([weights[i] for i in movable]), rest
        for i in movable:
            more = min(most - counts[i], max(1, budget * weights[i] // pool), rest)
            counts[i] = counts[i] + more
            rest = rest - more
    return np.array(counts)


def scatter_about(own_key, shape, width, reach, pieces=(), kind=jnp.bfloat16):
    factor_of = shard_levels(own_key, shape, pieces, -0.22, 0.18) if pieces else 1.0
    entries = jax.random.normal(own_key, shape, jnp.float32) * width * factor_of
    return jnp.minimum(jnp.maximum(entries, -reach), reach).astype(kind)


def heavy_noise(stream_key, shape, width, most, shards, heavy, held_as=jnp.bfloat16):
    array = width * jax.random.normal(stream_key, shape, jnp.float32)
    if shards:
        array = array * shard_levels(stream_key, shape, shards, -0.22, 0.18)
    return jnp.clip(with_spikes(array, jax.random.fold_in(stream_key, 3), *heavy), -most, most).astype(held_as)


def setup_inputs(seed: int = 0) -> dict:
    arg_keys = jax.random.split(jax.random.key(seed), 6)
    out_grad = heavy_noise(arg_keys[0], (TOKENS, D), 0.2, 1.1953125, ((0, 32),), (0, 1, 32, 2.75))
    saved_hidden = scatter_about(arg_keys[1], (TOKENS, TOPK, FF), 1.0, 6.0, ((0, 32),))
    gate_weight = jnp.clip(jnp.exp(math.log(1.0) - 1.6133518 * jax.random.uniform(arg_keys[2], (TOKENS, TOPK), jnp.float32) ** shard_levels(arg_keys[2], (TOKENS, TOPK), ((0, 32),), -0.2, 0.2)), 0.19921875, 1.0).astype(jnp.bfloat16)
    expert_ids_keys = jax.random.split(jax.random.fold_in(arg_keys[3], 1), TOKENS // TOK_DEV)
    expert_ids_turns = jax.random.permutation(jax.random.fold_in(arg_keys[3], 3), TOKENS // TOK_DEV)
    expert_ids = jax.vmap(lambda own, number: deal_out(jax.random.fold_in(arg_keys[3], 2), own, number, TOK_DEV, EXPERTS, TOPK, CAP, 2))(expert_ids_keys, expert_ids_turns).reshape((TOKENS, TOPK))
    down_weight = scatter_about(arg_keys[4], (D, EXPERTS, FF), FF ** -0.5, 0.3125, ((0, 4), (1, 8)))
    return dict(out_grad=out_grad, saved_hidden=saved_hidden, gate_weight=gate_weight, expert_ids=expert_ids, down_weight=down_weight)


def reference(out_grad, saved_hidden, gate_weight, expert_ids, down_weight):
    route_count = TOKENS * TOPK
    limit = CAP * N_DP * N_EXPERT
    flat_ids = expert_ids.reshape(route_count).astype(jnp.int32)
    grad_pad = jnp.concatenate([out_grad, jnp.zeros((1, D), out_grad.dtype)], axis=0)
    hidden_pad = jnp.concatenate([saved_hidden.reshape(route_count, FF), jnp.zeros((1, FF), saved_hidden.dtype)], axis=0)
    gate_pad = jnp.concatenate([gate_weight.reshape(route_count), jnp.zeros((1,), gate_weight.dtype)], axis=0)

    def one_expert(expert):
        routes = jnp.nonzero(flat_ids == expert, size=limit, fill_value=route_count)[0].astype(jnp.int32)
        token_rows = jnp.where(routes < route_count, routes // TOPK, TOKENS).astype(jnp.int32)
        grad_rows = grad_pad[token_rows]
        hidden_rows = hidden_pad[routes]
        gate_rows = gate_pad[routes]
        scaled = (grad_rows.astype(jnp.float32) * gate_rows.astype(jnp.float32)[:, None]).astype(jnp.bfloat16)
        weight = lax.dynamic_index_in_dim(down_weight, expert, 1, keepdims=False)
        weight_grad = jnp.dot(scaled.T, hidden_rows, preferred_element_type=jnp.float32)
        hidden_grad = jnp.dot(scaled, weight, preferred_element_type=jnp.float32).astype(jnp.bfloat16)
        recomputed = jnp.dot(hidden_rows, weight.T, preferred_element_type=jnp.float32)
        gate_grad = jnp.sum(grad_rows.astype(jnp.float32) * recomputed, axis=1).astype(jnp.bfloat16)
        return routes, hidden_grad, gate_grad, weight_grad

    routes, hidden_grads, gate_grads, weight_grads = lax.map(one_expert, jnp.arange(EXPERTS, dtype=jnp.int32))
    flat_routes = routes.reshape(EXPERTS * limit)
    grad_hidden = jnp.zeros((route_count + 1, FF), jnp.bfloat16).at[flat_routes].set(hidden_grads.reshape(EXPERTS * limit, FF))
    grad_hidden = grad_hidden[:route_count].reshape(TOKENS, TOPK, FF)
    grad_gate = jnp.zeros((route_count + 1,), jnp.bfloat16).at[flat_routes].set(gate_grads.reshape(EXPERTS * limit))
    grad_gate = grad_gate[:route_count].reshape(TOKENS, TOPK)
    grad_down = jnp.transpose(weight_grads, (1, 0, 2))
    return grad_hidden, grad_gate, grad_down
```

```python
import jax
import jax.numpy as jnp
from jax import lax
from jax.sharding import PartitionSpec as P


F32 = jnp.float32
BF16 = jnp.bfloat16


def swap(value, axis, shift):
    size = lax.axis_size(axis)
    return lax.ppermute(value, axis, [(i, i ^ shift) for i in range(size)])


def per_device(out_grad, saved_hidden, gate_weight, expert_ids, down_weight):
    tok_count, width = out_grad.shape
    top_count = expert_ids.shape[1]
    hidden_width = saved_hidden.shape[2]
    owners = lax.axis_size("expert")
    parts = lax.axis_size("dp")
    rows = width // parts
    local_experts = down_weight.shape[1]
    total_experts = local_experts * owners
    capacity = max(2, 3 * tok_count * top_count // (2 * total_experts))
    route_count = tok_count * top_count
    pair_slots = local_experts * capacity
    slot_count = owners * pair_slots
    wide = local_experts * hidden_width
    me = lax.axis_index("expert")
    my_part = lax.axis_index("dp")
    grid = parts == 4

    if grid:
        og = jnp.concatenate(
            [
                lax.dynamic_slice_in_dim(out_grad, (my_part ^ q) * rows, rows, axis=1)
                for q in range(parts)
            ],
            axis=1,
        )
    else:
        og = out_grad
    weight = down_weight.reshape(rows, wide)

    blocks = [None] * owners
    blocks[0] = og
    for r in range(2, owners, 2):
        blocks[r] = swap(og, "expert", r)
    if grid:
        wx = swap(weight, "dp", 1)
        wy = swap(weight, "dp", 2)

    rel = ((expert_ids // local_experts) ^ me) * local_experts + expert_ids % local_experts
    one_hot = rel[:, :, None] == jnp.arange(total_experts, dtype=jnp.int32)
    named = jnp.any(one_hot, axis=1)
    below = (
        jnp.arange(tok_count)[:, None] > jnp.arange(tok_count)[None, :]
    ).astype(BF16)
    position = jnp.dot(below, named.astype(BF16), preferred_element_type=F32)
    key = jnp.where(named, position, -1.0).astype(BF16)
    route_pos = jnp.sum(jnp.where(one_hot, position[:, None, :], 0.0), axis=2)
    slot = (rel * capacity + route_pos.astype(jnp.int32)).reshape(route_count)
    pick = (jnp.arange(slot_count, dtype=jnp.int32)[:, None] == slot[None, :]).astype(BF16)
    hidden = saved_hidden.reshape(route_count, hidden_width)
    gated = (saved_hidden.astype(F32) * gate_weight.astype(F32)[:, :, None]).astype(BF16)
    packed = jnp.dot(
        pick, gated.reshape(route_count, hidden_width), preferred_element_type=F32
    ).astype(BF16)
    key_rows = jnp.pad(
        key.T.reshape(owners, local_experts, tok_count),
        ((0, 0), (0, 16 - local_experts), (0, hidden_width - tok_count)),
    )
    packed = jnp.concatenate(
        [packed.reshape(owners, pair_slots, hidden_width), key_rows], axis=1
    )
    arrived = [packed[0]] + [swap(packed[r], "expert", r) for r in range(1, owners)]
    for r in range(0, owners, 2):
        blocks[r + 1] = swap(blocks[r], "expert", 1)
    if grid:
        half = rows // 2
        wd = jnp.concatenate(
            [swap(wy[:half], "dp", 1), swap(wx[half:], "dp", 2)], axis=0
        )
        full_weight = jnp.concatenate([weight, wx, wy, wd], axis=0)
    else:
        full_weight = lax.all_gather(weight, "dp", axis=0, tiled=True)

    places = jnp.arange(capacity, dtype=jnp.int32).astype(BF16)
    picks, spread = [], []
    for r in range(owners):
        key_in = arrived[r][pair_slots : pair_slots + local_experts, :tok_count]
        chosen = (key_in[:, None, :] == places[None, :, None]).astype(BF16)
        picks.append(chosen)
        slots_in = arrived[r][:pair_slots].reshape(local_experts, capacity, hidden_width)
        spread.append(
            jnp.concatenate(
                [
                    jnp.dot(chosen[e].T, slots_in[e], preferred_element_type=F32).astype(BF16)
                    for e in range(local_experts)
                ],
                axis=1,
            )
        )
    spread = jnp.concatenate(spread, axis=0)
    tokens = jnp.concatenate(blocks, axis=0)

    def weight_grad(q):
        return lax.dot_general(
            tokens[:, q * rows : (q + 1) * rows],
            spread,
            (((0,), (0,)), ((), ())),
            preferred_element_type=F32,
        )

    if grid:
        far = weight_grad(3).astype(BF16)
        far_x = swap(far[:half], "dp", 1)
        far_y = swap(far[half:], "dp", 2)
        near_x = weight_grad(1)
        near_y = weight_grad(2)
        own = weight_grad(0)
        near_y = jnp.concatenate([near_y[:half] + far_x.astype(F32), near_y[half:]], axis=0)
        near_x = jnp.concatenate([near_x[:half], near_x[half:] + far_y.astype(F32)], axis=0)
        from_x = swap(near_x.astype(BF16), "dp", 1)
        from_y = swap(near_y.astype(BF16), "dp", 2)
    else:
        partial = lax.dot_general(
            tokens, spread, (((0,), (0,)), ((), ())), preferred_element_type=F32
        ).astype(BF16)

    back = []
    for r in range(owners):
        dense = jnp.dot(blocks[r], full_weight, preferred_element_type=F32).astype(BF16)
        dense = dense.reshape(tok_count, local_experts, hidden_width)
        chosen = jnp.concatenate(
            [
                jnp.dot(picks[r][e], dense[:, e], preferred_element_type=F32).astype(BF16)
                for e in range(local_experts)
            ],
            axis=0,
        )
        back.append(chosen if r == 0 else swap(chosen, "expert", r))
    back = jnp.concatenate(back, axis=0)
    grad_act = lax.dot_general(
        pick, back, (((0,), (0,)), ((), ())), preferred_element_type=F32
    )
    grad_hidden = (
        grad_act.reshape(tok_count, top_count, hidden_width)
        * gate_weight.astype(F32)[:, :, None]
    ).astype(BF16)
    grad_gate = (
        jnp.sum(grad_act * hidden.astype(F32), axis=1)
        .reshape(tok_count, top_count)
        .astype(BF16)
    )
    if grid:
        grad_down = own + from_x.astype(F32) + from_y.astype(F32)
    else:
        grad_down = lax.psum_scatter(partial, "dp", scatter_dimension=0, tiled=True).astype(F32)
    return grad_hidden, grad_gate, grad_down.reshape(rows, local_experts, hidden_width)


def solution(mesh):
    in_specs = (
        P(("dp", "expert"), None),
        P(("dp", "expert"), None, None),
        P(("dp", "expert"), None),
        P(("dp", "expert"), None),
        P("dp", "expert", None),
    )
    out_specs = (
        P(("dp", "expert"), None, None),
        P(("dp", "expert"), None),
        P("dp", "expert", None),
    )
    return jax.shard_map(
        per_device, mesh=mesh, in_specs=in_specs, out_specs=out_specs, check_vma=False
    )
```

```python
import functools

import jax
import jax.numpy as jnp
from jax import lax
from jax.experimental import pallas as pl
from jax.experimental.pallas import tpu as pltpu
from jax.sharding import PartitionSpec as P


F32 = jnp.float32
BF16 = jnp.bfloat16


def swap(value, axis, shift):
    size = lax.axis_size(axis)
    return lax.ppermute(value, axis, [(i, i ^ shift) for i in range(size)])

MESH = pl.DeviceIdType.MESH
ORDER = (3, 1, 2, 0)
ON_ROWS = (((0,), (0,)), ((), ()))


def flip(value, shift):
    out, bit = value, 1
    while bit <= shift:
        if shift & bit:
            out = out + bit - 2 * bit * lax.rem(lax.div(value, bit), 2)
        bit *= 2
    return out


def matmul(a, b):
    return jnp.dot(a, b, preferred_element_type=F32)


def fused_kernel(
    dims,
    og_ref,
    hid_ref,
    gate_ref,
    ids_ref,
    w_ref,
    gh_ref,
    gg_ref,
    down_ref,
    toks,
    wrem,
    pick,
    gated,
    packed,
    arr,
    spread,
    far,
    far_in,
    near,
    near_out,
    near_in,
    dense,
    upack,
    back,
    og_send,
    og_recv,
    hs_send,
    hs_recv,
    u_send,
    u_recv,
    w_send,
    w_recv,
    g_send,
    g_recv,
):
    owners, local, cap, tok, top, ff = dims
    rows, wide = w_ref.shape
    half = rows // 2
    pair = local * cap
    slots = owners * pair
    me = lax.axis_index("expert")
    part = lax.axis_index("dp")

    barrier = pltpu.get_barrier_semaphore()
    for r in range(1, owners):
        pl.semaphore_signal(
            barrier, inc=1, device_id={"expert": flip(me, r)}, device_id_type=MESH
        )
    for q in (1, 2):
        pl.semaphore_signal(barrier, inc=1, device_id={"dp": flip(part, q)}, device_id_type=MESH)
    pl.semaphore_wait(barrier, owners + 1)

    def remote(source, target, send, recv, axis, shift):
        here = me if axis == "expert" else part
        return pltpu.make_async_remote_copy(
            src_ref=source,
            dst_ref=target,
            send_sem=send,
            recv_sem=recv,
            device_id={axis: flip(here, shift)},
            device_id_type=MESH,
        )

    low, high = pl.ds(0, half), pl.ds(half, half)
    w_moves = [
        remote(w_ref.at[high], wrem.at[0, high], w_send.at[0], w_recv.at[0], "dp", 1),
        remote(w_ref.at[low], wrem.at[1, low], w_send.at[1], w_recv.at[1], "dp", 2),
        remote(w_ref.at[low], wrem.at[0, low], w_send.at[2], w_recv.at[2], "dp", 1),
        remote(w_ref.at[high], wrem.at[1, high], w_send.at[3], w_recv.at[3], "dp", 2),
        remote(wrem.at[0, high], wrem.at[2, high], w_send.at[4], w_recv.at[4], "dp", 2),
        remote(wrem.at[1, low], wrem.at[2, low], w_send.at[5], w_recv.at[5], "dp", 1),
    ]
    for move in w_moves[:4]:
        move.start()

    def columns(q):
        return pl.ds(pl.multiple_of(flip(part, q) * rows, rows), rows)

    og_moves = {}
    for q in ORDER:
        for r in range(1, owners):
            if r == 1 or r % 2 == 0:
                source, shift = og_ref.at[:, columns(q)], r
            else:
                source, shift = toks.at[q, r - 1], 1
            og_moves[q, r] = remote(
                source, toks.at[q, r], og_send.at[q, r], og_recv.at[q, r], "expert", shift
            )

    def send_tokens(q):
        for r in (1,) + tuple(range(2, owners, 2)):
            og_moves[q, r].start()
        toks[q, 0] = og_ref[:, columns(q)]

    def pass_tokens(q):
        for r in range(2, owners, 2):
            og_moves[q, r].wait_recv()
            og_moves[q, r + 1].start()

    def have_tokens(q):
        for r in (1,) + tuple(range(3, owners, 2)):
            og_moves[q, r].wait_recv()

    send_tokens(ORDER[0])

    ids = ids_ref[...]
    group = lax.div(ids, local)
    rel = flip_value(group, me, owners) * local + lax.rem(ids, local)
    lanes = lax.broadcasted_iota(jnp.int32, (tok, tok), 1)
    subs = lax.broadcasted_iota(jnp.int32, (tok, tok), 0)
    named = jnp.zeros((tok, tok), F32)
    for k in range(top):
        named = jnp.where(rel[:, k : k + 1] == lanes, 1.0, named)
    below = jnp.where(subs > lanes, 1.0, 0.0).astype(BF16)
    unit = jnp.where(subs == lanes, 1.0, 0.0).astype(BF16)
    position = matmul(below, named.astype(BF16))
    key = jnp.where(named > 0.5, position, -1.0).astype(BF16)
    key_t = lax.dot_general(key, unit, ON_ROWS, preferred_element_type=F32)
    for r in range(owners):
        packed[r, pl.ds(pair, 16), :] = jnp.zeros((16, ff), BF16)
        packed[r, pl.ds(pair, 16), pl.ds(0, tok)] = key_t[r * local : r * local + 16].astype(BF16)
    slot_lanes = lax.broadcasted_iota(jnp.int32, (tok, slots), 1)
    for k in range(top):
        number = rel[:, k : k + 1]
        place = jnp.sum(jnp.where(number == lanes, position, 0.0), axis=1, keepdims=True)
        slot = number * cap + place.astype(jnp.int32)
        pick[pl.ds(k * tok, tok), :] = jnp.where(slot == slot_lanes, 1.0, 0.0).astype(BF16)
        gated[pl.ds(k * tok, tok), :] = (
            hid_ref[k].astype(F32) * gate_ref[:, k : k + 1]
        ).astype(BF16)
    for c in range(owners // 2):
        two = lax.dot_general(
            pick[:, pl.ds(c * 2 * pair, 2 * pair)],
            gated[...],
            ON_ROWS,
            preferred_element_type=F32,
        ).astype(BF16)
        packed[2 * c, pl.ds(0, pair), :] = two[:pair]
        packed[2 * c + 1, pl.ds(0, pair), :] = two[pair:]

    hs_moves = [None] + [
        remote(packed.at[r], arr.at[r], hs_send.at[r], hs_recv.at[r], "expert", r)
        for r in range(1, owners)
    ]
    for r in range(owners - 1, 0, -1):
        hs_moves[r].start()
    for q in ORDER[1:]:
        send_tokens(q)
    arr[0] = packed[0]

    pass_tokens(ORDER[0])
    w_moves[0].wait_recv()
    w_moves[4].start()
    w_moves[1].wait_recv()
    w_moves[5].start()

    places = lax.broadcasted_iota(jnp.int32, (cap, tok), 0).astype(F32)

    def chosen(r, e):
        row = arr[r, pl.ds(pair, 16), pl.ds(0, tok)].astype(F32)[e : e + 1]
        return jnp.where(row == places, 1.0, 0.0).astype(BF16)

    for r in range(owners):
        if r:
            hs_moves[r].wait_recv()
        for e in range(local):
            spread[pl.ds(r * tok, tok), pl.ds(e * ff, ff)] = lax.dot_general(
                chosen(r, e),
                arr[r, pl.ds(e * cap, cap), :],
                ON_ROWS,
                preferred_element_type=F32,
            ).astype(BF16)

    def weight_grad(q, store):
        @pl.loop(0, local)
        def _(e):
            at = pl.ds(pl.multiple_of(e * ff, ff), ff)
            store(
                at,
                lax.dot_general(
                    toks[q].reshape(owners * tok, rows),
                    spread[:, at],
                    ON_ROWS,
                    preferred_element_type=F32,
                ),
            )

    def keep_far(at, value):
        far[:, at] = value.astype(BF16)

    have_tokens(3)
    weight_grad(3, keep_far)
    far_moves = [
        remote(far.at[low], far_in.at[0], g_send.at[0], g_recv.at[0], "dp", 1),
        remote(far.at[high], far_in.at[1], g_send.at[1], g_recv.at[1], "dp", 2),
    ]
    for move in far_moves:
        move.start()
    first = {1: low, 2: high}
    last = {1: high, 2: low}
    near_moves = {}
    for q in (1, 2):
        for n, span in enumerate((first[q], last[q])):
            i = 2 * q + n
            near_moves[q, n] = remote(
                near_out.at[q - 1, span],
                near_in.at[q - 1, span],
                g_send.at[i],
                g_recv.at[i],
                "dp",
                q,
            )
    for q in (1, 2):
        pass_tokens(q)
        have_tokens(q)

        def keep_near(at, value):
            near[q - 1, :, at] = value[half:] if q == 1 else value[:half]
            free = value[:half] if q == 1 else value[half:]
            near_out[q - 1, first[q], at] = free.astype(BF16)

        weight_grad(q, keep_near)
        near_moves[q, 0].start()
    pass_tokens(0)
    have_tokens(0)

    def close(q):
        far_moves[2 - q].wait_recv()
        near_out[q - 1, last[q], :] = (near[q - 1] + far_in[2 - q].astype(F32)).astype(BF16)
        near_moves[q, 1].start()

    close(2)
    close(1)
    for i in (2, 3, 4, 5):
        w_moves[i].wait_recv()

    u_moves = [None] + [
        remote(upack.at[r], back.at[r], u_send.at[r], u_recv.at[r], "expert", r)
        for r in range(1, owners)
    ]
    group_size = owners // 2
    for g in (1, 0):
        span = pl.ds(g * group_size, group_size)

        @pl.loop(0, local)
        def _(e):
            at = pl.ds(pl.multiple_of(e * ff, ff), ff)
            total = matmul(toks[0, span].reshape(group_size * tok, rows), w_ref[:, at])
            for q in (1, 2, 3):
                total += matmul(
                    toks[q, span].reshape(group_size * tok, rows), wrem[q - 1, :, at]
                )
            dense[:, at] = total.astype(BF16)

        for i in range(group_size - 1, -1, -1):
            r = g * group_size + i
            for e in range(local):
                value = matmul(
                    chosen(r, e), dense[pl.ds(i * tok, tok), pl.ds(e * ff, ff)]
                ).astype(BF16)
                if r:
                    upack[r, pl.ds(e * cap, cap), :] = value
                else:
                    back[0, pl.ds(e * cap, cap), :] = value
            if r:
                u_moves[r].start()

    def keep_own(at, value):
        down_ref[:, at] = value

    weight_grad(0, keep_own)

    for r in range(1, owners):
        u_moves[r].wait_recv()
    gate_lanes = lax.broadcasted_iota(jnp.int32, (tok, tok), 1)
    totals = jnp.zeros((tok, tok), F32)
    every = back[...].reshape(slots, ff)
    for k in range(0, top, 2):
        acts = matmul(pick[pl.ds(k * tok, 2 * tok), :], every)
        for j in range(2):
            act = acts[j * tok : (j + 1) * tok]
            gh_ref[k + j] = (act * gate_ref[:, k + j : k + j + 1]).astype(BF16)
            dot = jnp.sum(act * hid_ref[k + j].astype(F32), axis=1, keepdims=True)
            totals = jnp.where(gate_lanes == k + j, dot, totals)
    gg_ref[...] = totals

    for q in (1, 2):
        for n in (0, 1):
            near_moves[q, n].wait_recv()
    down_ref[...] += near_in[0].astype(F32) + near_in[1].astype(F32)

    for move in w_moves + far_moves + hs_moves[1:] + u_moves[1:]:
        move.wait_send()
    for move in list(near_moves.values()) + list(og_moves.values()):
        move.wait_send()


def flip_value(group, me, owners):
    out, bit = group, 1
    while bit < owners:
        mine = lax.rem(lax.div(me, bit), 2)
        theirs = lax.rem(lax.div(group, bit), 2)
        out = out + bit * mine * (1 - 2 * theirs)
        bit *= 2
    return out


def fused(out_grad, saved_hidden, gate_weight, expert_ids, down_weight):
    tok, width = out_grad.shape
    top, ff = saved_hidden.shape[1:]
    owners = lax.axis_size("expert")
    rows, local = down_weight.shape[:2]
    wide = local * ff
    cap = max(2, 3 * tok * top // (2 * local * owners))
    pair = local * cap
    half = rows // 2
    dims = (owners, local, cap, tok, top, ff)
    vmem = pl.BlockSpec(memory_space=pltpu.VMEM)
    dma = pltpu.SemaphoreType.DMA
    grad_act, totals, grad_down = pl.pallas_call(
        functools.partial(fused_kernel, dims),
        out_shape=(
            jax.ShapeDtypeStruct((top, tok, ff), BF16),
            jax.ShapeDtypeStruct((tok, tok), F32),
            jax.ShapeDtypeStruct((rows, wide), F32),
        ),
        in_specs=[vmem] * 5,
        out_specs=(vmem,) * 3,
        scratch_shapes=[
            pltpu.VMEM((4, owners, tok, rows), BF16),
            pltpu.VMEM((3, rows, wide), BF16),
            pltpu.VMEM((top * tok, owners * pair), BF16),
            pltpu.VMEM((top * tok, ff), BF16),
            pltpu.VMEM((owners, pair + 16, ff), BF16),
            pltpu.VMEM((owners, pair + 16, ff), BF16),
            pltpu.VMEM((owners * tok, wide), BF16),
            pltpu.VMEM((rows, wide), BF16),
            pltpu.VMEM((2, half, wide), BF16),
            pltpu.VMEM((2, half, wide), F32),
            pltpu.VMEM((2, rows, wide), BF16),
            pltpu.VMEM((2, rows, wide), BF16),
            pltpu.VMEM((owners // 2 * tok, wide), BF16),
            pltpu.VMEM((owners, pair, ff), BF16),
            pltpu.VMEM((owners, pair, ff), BF16),
            dma((4, owners)),
            dma((4, owners)),
            dma((owners,)),
            dma((owners,)),
            dma((owners,)),
            dma((owners,)),
            dma((6,)),
            dma((6,)),
            dma((6,)),
            dma((6,)),
        ],
        compiler_params=pltpu.CompilerParams(
            collective_id=0, has_side_effects=True, vmem_limit_bytes=62 << 20
        ),
    )(
        out_grad,
        jnp.transpose(saved_hidden, (1, 0, 2)),
        gate_weight.astype(F32),
        expert_ids,
        down_weight.reshape(rows, wide),
    )
    return (
        jnp.transpose(grad_act, (1, 0, 2)),
        totals[:, :top].astype(BF16),
        grad_down.reshape(rows, local, ff),
    )


def per_device(out_grad, saved_hidden, gate_weight, expert_ids, down_weight):
    if lax.axis_size("dp") == 4 and lax.axis_size("expert") == 8:
        return fused(out_grad, saved_hidden, gate_weight, expert_ids, down_weight)
    tok_count, width = out_grad.shape
    top_count = expert_ids.shape[1]
    hidden_width = saved_hidden.shape[2]
    owners = lax.axis_size("expert")
    parts = lax.axis_size("dp")
    rows = width // parts
    local_experts = down_weight.shape[1]
    total_experts = local_experts * owners
    capacity = max(2, 3 * tok_count * top_count // (2 * total_experts))
    route_count = tok_count * top_count
    pair_slots = local_experts * capacity
    slot_count = owners * pair_slots
    wide = local_experts * hidden_width
    me = lax.axis_index("expert")
    my_part = lax.axis_index("dp")
    grid = parts == 4

    if grid:
        og = jnp.concatenate(
            [
                lax.dynamic_slice_in_dim(out_grad, (my_part ^ q) * rows, rows, axis=1)
                for q in range(parts)
            ],
            axis=1,
        )
    else:
        og = out_grad
    weight = down_weight.reshape(rows, wide)

    blocks = [None] * owners
    blocks[0] = og
    for r in range(2, owners, 2):
        blocks[r] = swap(og, "expert", r)
    if grid:
        wx = swap(weight, "dp", 1)
        wy = swap(weight, "dp", 2)

    rel = ((expert_ids // local_experts) ^ me) * local_experts + expert_ids % local_experts
    one_hot = rel[:, :, None] == jnp.arange(total_experts, dtype=jnp.int32)
    named = jnp.any(one_hot, axis=1)
    below = (
        jnp.arange(tok_count)[:, None] > jnp.arange(tok_count)[None, :]
    ).astype(BF16)
    position = jnp.dot(below, named.astype(BF16), preferred_element_type=F32)
    key = jnp.where(named, position, -1.0).astype(BF16)
    route_pos = jnp.sum(jnp.where(one_hot, position[:, None, :], 0.0), axis=2)
    slot = (rel * capacity + route_pos.astype(jnp.int32)).reshape(route_count)
    pick = (jnp.arange(slot_count, dtype=jnp.int32)[:, None] == slot[None, :]).astype(BF16)
    hidden = saved_hidden.reshape(route_count, hidden_width)
    gated = (saved_hidden.astype(F32) * gate_weight.astype(F32)[:, :, None]).astype(BF16)
    packed = jnp.dot(
        pick, gated.reshape(route_count, hidden_width), preferred_element_type=F32
    ).astype(BF16)
    key_rows = jnp.pad(
        key.T.reshape(owners, local_experts, tok_count),
        ((0, 0), (0, 16 - local_experts), (0, hidden_width - tok_count)),
    )
    packed = jnp.concatenate(
        [packed.reshape(owners, pair_slots, hidden_width), key_rows], axis=1
    )
    arrived = [packed[0]] + [swap(packed[r], "expert", r) for r in range(1, owners)]
    for r in range(0, owners, 2):
        blocks[r + 1] = swap(blocks[r], "expert", 1)
    if grid:
        half = rows // 2
        wd = jnp.concatenate(
            [swap(wy[:half], "dp", 1), swap(wx[half:], "dp", 2)], axis=0
        )
        full_weight = jnp.concatenate([weight, wx, wy, wd], axis=0)
    else:
        full_weight = lax.all_gather(weight, "dp", axis=0, tiled=True)

    places = jnp.arange(capacity, dtype=jnp.int32).astype(BF16)
    picks, spread = [], []
    for r in range(owners):
        key_in = arrived[r][pair_slots : pair_slots + local_experts, :tok_count]
        chosen = (key_in[:, None, :] == places[None, :, None]).astype(BF16)
        picks.append(chosen)
        slots_in = arrived[r][:pair_slots].reshape(local_experts, capacity, hidden_width)
        spread.append(
            jnp.concatenate(
                [
                    jnp.dot(chosen[e].T, slots_in[e], preferred_element_type=F32).astype(BF16)
                    for e in range(local_experts)
                ],
                axis=1,
            )
        )
    spread = jnp.concatenate(spread, axis=0)
    tokens = jnp.concatenate(blocks, axis=0)

    def weight_grad(q):
        return lax.dot_general(
            tokens[:, q * rows : (q + 1) * rows],
            spread,
            (((0,), (0,)), ((), ())),
            preferred_element_type=F32,
        )

    if grid:
        far = weight_grad(3).astype(BF16)
        far_x = swap(far[:half], "dp", 1)
        far_y = swap(far[half:], "dp", 2)
        near_x = weight_grad(1)
        near_y = weight_grad(2)
        own = weight_grad(0)
        near_y = jnp.concatenate([near_y[:half] + far_x.astype(F32), near_y[half:]], axis=0)
        near_x = jnp.concatenate([near_x[:half], near_x[half:] + far_y.astype(F32)], axis=0)
        from_x = swap(near_x.astype(BF16), "dp", 1)
        from_y = swap(near_y.astype(BF16), "dp", 2)
    else:
        partial = lax.dot_general(
            tokens, spread, (((0,), (0,)), ((), ())), preferred_element_type=F32
        ).astype(BF16)

    back = []
    for r in range(owners):
        dense = jnp.dot(blocks[r], full_weight, preferred_element_type=F32).astype(BF16)
        dense = dense.reshape(tok_count, local_experts, hidden_width)
        chosen = jnp.concatenate(
            [
                jnp.dot(picks[r][e], dense[:, e], preferred_element_type=F32).astype(BF16)
                for e in range(local_experts)
            ],
            axis=0,
        )
        back.append(chosen if r == 0 else swap(chosen, "expert", r))
    back = jnp.concatenate(back, axis=0)
    grad_act = lax.dot_general(
        pick, back, (((0,), (0,)), ((), ())), preferred_element_type=F32
    )
    grad_hidden = (
        grad_act.reshape(tok_count, top_count, hidden_width)
        * gate_weight.astype(F32)[:, :, None]
    ).astype(BF16)
    grad_gate = (
        jnp.sum(grad_act * hidden.astype(F32), axis=1)
        .reshape(tok_count, top_count)
        .astype(BF16)
    )
    if grid:
        grad_down = own + from_x.astype(F32) + from_y.astype(F32)
    else:
        grad_down = lax.psum_scatter(partial, "dp", scatter_dimension=0, tiled=True).astype(F32)
    return grad_hidden, grad_gate, grad_down.reshape(rows, local_experts, hidden_width)


def solution(mesh):
    in_specs = (
        P(("dp", "expert"), None),
        P(("dp", "expert"), None, None),
        P(("dp", "expert"), None),
        P(("dp", "expert"), None),
        P("dp", "expert", None),
    )
    out_specs = (
        P(("dp", "expert"), None, None),
        P(("dp", "expert"), None),
        P("dp", "expert", None),
    )
    return jax.shard_map(
        per_device, mesh=mesh, in_specs=in_specs, out_specs=out_specs, check_vma=False
    )
```

```python
import functools

import jax
import jax.numpy as jnp
from jax import lax
from jax.experimental import pallas as pl
from jax.experimental.pallas import tpu as pltpu
from jax.sharding import PartitionSpec as P


F32 = jnp.float32
BF16 = jnp.bfloat16


def swap(value, axis, shift):
    size = lax.axis_size(axis)
    return lax.ppermute(value, axis, [(i, i ^ shift) for i in range(size)])

MESH = pl.DeviceIdType.MESH
ORDER = (3, 1, 2, 0)
ON_ROWS = (((0,), (0,)), ((), ()))


def flip(value, shift):
    out, bit = value, 1
    while bit <= shift:
        if shift & bit:
            out = out + bit - 2 * bit * lax.rem(lax.div(value, bit), 2)
        bit *= 2
    return out


def matmul(a, b):
    return jnp.dot(a, b, preferred_element_type=F32)


def fused_kernel(
    dims,
    og_ref,
    hid_ref,
    gate_ref,
    ids_ref,
    w_ref,
    gh_ref,
    gg_ref,
    down_ref,
    toks,
    wrem,
    pick,
    gated,
    packed,
    arr,
    spread,
    far,
    far_in,
    near,
    near_out,
    near_in,
    dense,
    upack,
    back,
    gate_col,
    og_send,
    og_recv,
    hs_send,
    hs_recv,
    u_send,
    u_recv,
    w_send,
    w_recv,
    g_send,
    g_recv,
):
    owners, local, cap, tok, top, ff = dims
    rows, wide = w_ref.shape
    half = rows // 2
    pair = local * cap
    slots = owners * pair
    me = lax.axis_index("expert")
    part = lax.axis_index("dp")

    barrier = pltpu.get_barrier_semaphore()
    for r in range(1, owners):
        pl.semaphore_signal(
            barrier, inc=1, device_id={"expert": flip(me, r)}, device_id_type=MESH
        )
    for q in (1, 2):
        pl.semaphore_signal(barrier, inc=1, device_id={"dp": flip(part, q)}, device_id_type=MESH)
    pl.semaphore_wait(barrier, owners + 1)

    def remote(source, target, send, recv, axis, shift):
        here = me if axis == "expert" else part
        return pltpu.make_async_remote_copy(
            src_ref=source,
            dst_ref=target,
            send_sem=send,
            recv_sem=recv,
            device_id={axis: flip(here, shift)},
            device_id_type=MESH,
        )

    low, high = pl.ds(0, half), pl.ds(half, half)
    w_moves = [
        remote(w_ref.at[high], wrem.at[0, high], w_send.at[0], w_recv.at[0], "dp", 1),
        remote(w_ref.at[low], wrem.at[1, low], w_send.at[1], w_recv.at[1], "dp", 2),
        remote(w_ref.at[low], wrem.at[0, low], w_send.at[2], w_recv.at[2], "dp", 1),
        remote(w_ref.at[high], wrem.at[1, high], w_send.at[3], w_recv.at[3], "dp", 2),
        remote(wrem.at[0, high], wrem.at[2, high], w_send.at[4], w_recv.at[4], "dp", 2),
        remote(wrem.at[1, low], wrem.at[2, low], w_send.at[5], w_recv.at[5], "dp", 1),
    ]
    for move in w_moves[:4]:
        move.start()

    def columns(q):
        return pl.ds(pl.multiple_of(flip(part, q) * rows, rows), rows)

    og_moves = {}
    for q in ORDER:
        for r in range(1, owners):
            if r == 1 or r % 2 == 0:
                source, shift = og_ref.at[:, columns(q)], r
            else:
                source, shift = toks.at[q, r - 1], 1
            og_moves[q, r] = remote(
                source, toks.at[q, r], og_send.at[q, r], og_recv.at[q, r], "expert", shift
            )

    def send_tokens(q):
        for r in (1,) + tuple(range(2, owners, 2)):
            og_moves[q, r].start()
        toks[q, 0] = og_ref[:, columns(q)]

    def pass_tokens(q):
        for r in range(2, owners, 2):
            og_moves[q, r].wait_recv()
            og_moves[q, r + 1].start()

    def have_tokens(q):
        for r in (1,) + tuple(range(3, owners, 2)):
            og_moves[q, r].wait_recv()

    send_tokens(ORDER[0])

    lanes = lax.broadcasted_iota(jnp.int32, (tok, tok), 1)
    subs = lax.broadcasted_iota(jnp.int32, (tok, tok), 0)
    below = jnp.where(subs > lanes, 1.0, 0.0).astype(BF16)
    unit = jnp.where(subs == lanes, 1.0, 0.0).astype(BF16)
    both = jnp.concatenate([ids_ref[...].astype(F32), gate_ref[...].astype(F32)], axis=0)
    upright = lax.dot_general(
        both.astype(BF16), unit[: 2 * top], ON_ROWS, preferred_element_type=F32
    )
    ids = upright[:, :top].astype(jnp.int32)
    rel = flip_value(lax.div(ids, local), me, owners) * local + lax.rem(ids, local)
    named = jnp.zeros((tok, tok), F32)
    for k in range(top):
        named = jnp.where(rel[:, k : k + 1] == lanes, 1.0, named)
    position = matmul(below, named.astype(BF16))
    key = jnp.where(named > 0.5, position, -1.0).astype(BF16)
    key_t = lax.dot_general(key, unit, ON_ROWS, preferred_element_type=F32)
    for r in range(owners):
        packed[r, pl.ds(pair, 16), :] = jnp.zeros((16, ff), BF16)
        packed[r, pl.ds(pair, 16), pl.ds(0, tok)] = key_t[r * local : r * local + 16].astype(BF16)
    table = jnp.zeros((tok, tok), F32)
    for k in range(top):
        number = rel[:, k : k + 1]
        place = jnp.sum(jnp.where(number == lanes, position, 0.0), axis=1, keepdims=True)
        table = jnp.where(lanes == k, number.astype(F32), table)
        table = jnp.where(lanes == top + k, place, table)
        table = jnp.where(lanes == 2 * top + k, upright[:, top + k : top + k + 1], table)
    table = table.astype(BF16)
    slot_lanes = lax.broadcasted_iota(jnp.int32, (tok, slots), 1)
    turn = lax.rem(subs, top)
    for c in range(top):
        span = pl.ds(c * tok, tok)
        start = (lanes - c * (tok // top)) * top
        spot = jnp.where((subs >= start) & (subs < start + top), 1.0, 0.0).astype(BF16)
        shown = matmul(spot, table)

        def pull(offset):
            return jnp.sum(jnp.where(lanes == turn + offset, shown, 0.0), axis=1, keepdims=True)

        slot = (pull(0) * cap + pull(top)).astype(jnp.int32)
        pick[span, :] = jnp.where(slot == slot_lanes, 1.0, 0.0).astype(BF16)
        gates = pull(2 * top)
        gate_col[span, :] = jnp.broadcast_to(gates, (tok, tok))
        gated[span, :] = (hid_ref[span, :].astype(F32) * gates).astype(BF16)
    for c in range(owners // 2):
        two = lax.dot_general(
            pick[:, pl.ds(c * 2 * pair, 2 * pair)],
            gated[...],
            ON_ROWS,
            preferred_element_type=F32,
        ).astype(BF16)
        packed[2 * c, pl.ds(0, pair), :] = two[:pair]
        packed[2 * c + 1, pl.ds(0, pair), :] = two[pair:]

    hs_moves = [None] + [
        remote(packed.at[r], arr.at[r], hs_send.at[r], hs_recv.at[r], "expert", r)
        for r in range(1, owners)
    ]
    for r in range(owners - 1, 0, -1):
        hs_moves[r].start()
    for q in ORDER[1:]:
        send_tokens(q)
    arr[0] = packed[0]

    pass_tokens(ORDER[0])
    w_moves[0].wait_recv()
    w_moves[4].start()
    w_moves[1].wait_recv()
    w_moves[5].start()

    places = lax.broadcasted_iota(jnp.int32, (cap, tok), 0).astype(F32)

    def chosen(r, e):
        row = arr[r, pl.ds(pair, 16), pl.ds(0, tok)].astype(F32)[e : e + 1]
        return jnp.where(row == places, 1.0, 0.0).astype(BF16)

    for r in range(owners):
        if r:
            hs_moves[r].wait_recv()
        for e in range(local):
            spread[pl.ds(r * tok, tok), pl.ds(e * ff, ff)] = lax.dot_general(
                chosen(r, e),
                arr[r, pl.ds(e * cap, cap), :],
                ON_ROWS,
                preferred_element_type=F32,
            ).astype(BF16)

    def weight_grad(q, store):
        @pl.loop(0, local)
        def _(e):
            at = pl.ds(pl.multiple_of(e * ff, ff), ff)
            store(
                at,
                lax.dot_general(
                    toks[q].reshape(owners * tok, rows),
                    spread[:, at],
                    ON_ROWS,
                    preferred_element_type=F32,
                ),
            )

    def keep_far(at, value):
        far[:, at] = value.astype(BF16)

    have_tokens(3)
    weight_grad(3, keep_far)
    far_moves = [
        remote(far.at[low], far_in.at[0], g_send.at[0], g_recv.at[0], "dp", 1),
        remote(far.at[high], far_in.at[1], g_send.at[1], g_recv.at[1], "dp", 2),
    ]
    for move in far_moves:
        move.start()
    first = {1: low, 2: high}
    last = {1: high, 2: low}
    near_moves = {}
    for q in (1, 2):
        for n, span in enumerate((first[q], last[q])):
            i = 2 * q + n
            near_moves[q, n] = remote(
                near_out.at[q - 1, span],
                near_in.at[q - 1, span],
                g_send.at[i],
                g_recv.at[i],
                "dp",
                q,
            )
    for q in (1, 2):
        pass_tokens(q)
        have_tokens(q)

        def keep_near(at, value):
            near[q - 1, :, at] = value[half:] if q == 1 else value[:half]
            free = value[:half] if q == 1 else value[half:]
            near_out[q - 1, first[q], at] = free.astype(BF16)

        weight_grad(q, keep_near)
        near_moves[q, 0].start()
    pass_tokens(0)
    have_tokens(0)

    def close(q):
        far_moves[2 - q].wait_recv()
        near_out[q - 1, last[q], :] = (near[q - 1] + far_in[2 - q].astype(F32)).astype(BF16)
        near_moves[q, 1].start()

    for i in (2, 3, 4, 5):
        w_moves[i].wait_recv()

    u_moves = [None] + [
        remote(upack.at[r], back.at[r], u_send.at[r], u_recv.at[r], "expert", r)
        for r in range(1, owners)
    ]
    group_size = owners // 2
    for g in (1, 0):
        span = pl.ds(g * group_size, group_size)

        @pl.loop(0, local)
        def _(e):
            at = pl.ds(pl.multiple_of(e * ff, ff), ff)
            total = matmul(toks[0, span].reshape(group_size * tok, rows), w_ref[:, at])
            for q in (1, 2, 3):
                total += matmul(
                    toks[q, span].reshape(group_size * tok, rows), wrem[q - 1, :, at]
                )
            dense[:, at] = total.astype(BF16)

        for i in range(group_size - 1, -1, -1):
            r = g * group_size + i
            for e in range(local):
                value = matmul(
                    chosen(r, e), dense[pl.ds(i * tok, tok), pl.ds(e * ff, ff)]
                ).astype(BF16)
                if r:
                    upack[r, pl.ds(e * cap, cap), :] = value
                else:
                    back[0, pl.ds(e * cap, cap), :] = value
            if r:
                u_moves[r].start()
        if g:
            close(2)
            close(1)

    def keep_own(at, value):
        down_ref[:, at] = value

    weight_grad(0, keep_own)

    for r in range(1, owners):
        u_moves[r].wait_recv()
    every = back[...].reshape(slots, ff)
    totals = []
    for c in range(0, top, 2):
        acts = matmul(pick[pl.ds(c * tok, 2 * tok), :], every)
        for j in range(2):
            span = pl.ds((c + j) * tok, tok)
            act = acts[j * tok : (j + 1) * tok]
            gh_ref[span, :] = (act * gate_col[span, 0:1]).astype(BF16)
            dot = jnp.sum(act * hid_ref[span, :].astype(F32), axis=1, keepdims=True)
            dot = jnp.where(lanes == turn, dot, 0.0)
            totals.append(jnp.sum(dot.reshape(tok // top, top, tok), axis=1))
    gg_ref[...] = jnp.transpose(jnp.concatenate(totals, axis=0))[:top]

    for q in (1, 2):
        for n in (0, 1):
            near_moves[q, n].wait_recv()
    down_ref[...] += near_in[0].astype(F32) + near_in[1].astype(F32)

    for move in w_moves + far_moves + hs_moves[1:] + u_moves[1:]:
        move.wait_send()
    for move in list(near_moves.values()) + list(og_moves.values()):
        move.wait_send()


def flip_value(group, me, owners):
    out, bit = group, 1
    while bit < owners:
        mine = lax.rem(lax.div(me, bit), 2)
        theirs = lax.rem(lax.div(group, bit), 2)
        out = out + bit * mine * (1 - 2 * theirs)
        bit *= 2
    return out


def fused(out_grad, saved_hidden, gate_weight, expert_ids, down_weight):
    tok, width = out_grad.shape
    top, ff = saved_hidden.shape[1:]
    owners = lax.axis_size("expert")
    rows, local = down_weight.shape[:2]
    wide = local * ff
    cap = max(2, 3 * tok * top // (2 * local * owners))
    pair = local * cap
    half = rows // 2
    dims = (owners, local, cap, tok, top, ff)
    vmem = pl.BlockSpec(memory_space=pltpu.VMEM)
    dma = pltpu.SemaphoreType.DMA
    grad_act, totals, grad_down = pl.pallas_call(
        functools.partial(fused_kernel, dims),
        out_shape=(
            jax.ShapeDtypeStruct((top * tok, ff), BF16),
            jax.ShapeDtypeStruct((top, tok), F32),
            jax.ShapeDtypeStruct((rows, wide), F32),
        ),
        in_specs=[vmem] * 5,
        out_specs=(vmem,) * 3,
        scratch_shapes=[
            pltpu.VMEM((4, owners, tok, rows), BF16),
            pltpu.VMEM((3, rows, wide), BF16),
            pltpu.VMEM((top * tok, owners * pair), BF16),
            pltpu.VMEM((top * tok, ff), BF16),
            pltpu.VMEM((owners, pair + 16, ff), BF16),
            pltpu.VMEM((owners, pair + 16, ff), BF16),
            pltpu.VMEM((owners * tok, wide), BF16),
            pltpu.VMEM((rows, wide), BF16),
            pltpu.VMEM((2, half, wide), BF16),
            pltpu.VMEM((2, half, wide), F32),
            pltpu.VMEM((2, rows, wide), BF16),
            pltpu.VMEM((2, rows, wide), BF16),
            pltpu.VMEM((owners // 2 * tok, wide), BF16),
            pltpu.VMEM((owners, pair, ff), BF16),
            pltpu.VMEM((owners, pair, ff), BF16),
            pltpu.VMEM((top * tok, tok), F32),
            dma((4, owners)),
            dma((4, owners)),
            dma((owners,)),
            dma((owners,)),
            dma((owners,)),
            dma((owners,)),
            dma((6,)),
            dma((6,)),
            dma((6,)),
            dma((6,)),
        ],
        compiler_params=pltpu.CompilerParams(
            collective_id=0, has_side_effects=True, vmem_limit_bytes=62 << 20
        ),
    )(
        out_grad,
        saved_hidden.reshape(tok * top, ff),
        gate_weight.T,
        expert_ids.T,
        down_weight.reshape(rows, wide),
    )
    return (
        grad_act.reshape(tok, top, ff),
        totals.T.astype(BF16),
        grad_down.reshape(rows, local, ff),
    )


def per_device(out_grad, saved_hidden, gate_weight, expert_ids, down_weight):
    if lax.axis_size("dp") == 4 and lax.axis_size("expert") == 8:
        return fused(out_grad, saved_hidden, gate_weight, expert_ids, down_weight)
    tok_count, width = out_grad.shape
    top_count = expert_ids.shape[1]
    hidden_width = saved_hidden.shape[2]
    owners = lax.axis_size("expert")
    parts = lax.axis_size("dp")
    rows = width // parts
    local_experts = down_weight.shape[1]
    total_experts = local_experts * owners
    capacity = max(2, 3 * tok_count * top_count // (2 * total_experts))
    route_count = tok_count * top_count
    pair_slots = local_experts * capacity
    slot_count = owners * pair_slots
    wide = local_experts * hidden_width
    me = lax.axis_index("expert")
    my_part = lax.axis_index("dp")
    grid = parts == 4

    if grid:
        og = jnp.concatenate(
            [
                lax.dynamic_slice_in_dim(out_grad, (my_part ^ q) * rows, rows, axis=1)
                for q in range(parts)
            ],
            axis=1,
        )
    else:
        og = out_grad
    weight = down_weight.reshape(rows, wide)

    blocks = [None] * owners
    blocks[0] = og
    for r in range(2, owners, 2):
        blocks[r] = swap(og, "expert", r)
    if grid:
        wx = swap(weight, "dp", 1)
        wy = swap(weight, "dp", 2)

    rel = ((expert_ids // local_experts) ^ me) * local_experts + expert_ids % local_experts
    one_hot = rel[:, :, None] == jnp.arange(total_experts, dtype=jnp.int32)
    named = jnp.any(one_hot, axis=1)
    below = (
        jnp.arange(tok_count)[:, None] > jnp.arange(tok_count)[None, :]
    ).astype(BF16)
    position = jnp.dot(below, named.astype(BF16), preferred_element_type=F32)
    key = jnp.where(named, position, -1.0).astype(BF16)
    route_pos = jnp.sum(jnp.where(one_hot, position[:, None, :], 0.0), axis=2)
    slot = (rel * capacity + route_pos.astype(jnp.int32)).reshape(route_count)
    pick = (jnp.arange(slot_count, dtype=jnp.int32)[:, None] == slot[None, :]).astype(BF16)
    hidden = saved_hidden.reshape(route_count, hidden_width)
    gated = (saved_hidden.astype(F32) * gate_weight.astype(F32)[:, :, None]).astype(BF16)
    packed = jnp.dot(
        pick, gated.reshape(route_count, hidden_width), preferred_element_type=F32
    ).astype(BF16)
    key_rows = jnp.pad(
        key.T.reshape(owners, local_experts, tok_count),
        ((0, 0), (0, 16 - local_experts), (0, hidden_width - tok_count)),
    )
    packed = jnp.concatenate(
        [packed.reshape(owners, pair_slots, hidden_width), key_rows], axis=1
    )
    arrived = [packed[0]] + [swap(packed[r], "expert", r) for r in range(1, owners)]
    for r in range(0, owners, 2):
        blocks[r + 1] = swap(blocks[r], "expert", 1)
    if grid:
        half = rows // 2
        wd = jnp.concatenate(
            [swap(wy[:half], "dp", 1), swap(wx[half:], "dp", 2)], axis=0
        )
        full_weight = jnp.concatenate([weight, wx, wy, wd], axis=0)
    else:
        full_weight = lax.all_gather(weight, "dp", axis=0, tiled=True)

    places = jnp.arange(capacity, dtype=jnp.int32).astype(BF16)
    picks, spread = [], []
    for r in range(owners):
        key_in = arrived[r][pair_slots : pair_slots + local_experts, :tok_count]
        chosen = (key_in[:, None, :] == places[None, :, None]).astype(BF16)
        picks.append(chosen)
        slots_in = arrived[r][:pair_slots].reshape(local_experts, capacity, hidden_width)
        spread.append(
            jnp.concatenate(
                [
                    jnp.dot(chosen[e].T, slots_in[e], preferred_element_type=F32).astype(BF16)
                    for e in range(local_experts)
                ],
                axis=1,
            )
        )
    spread = jnp.concatenate(spread, axis=0)
    tokens = jnp.concatenate(blocks, axis=0)

    def weight_grad(q):
        return lax.dot_general(
            tokens[:, q * rows : (q + 1) * rows],
            spread,
            (((0,), (0,)), ((), ())),
            preferred_element_type=F32,
        )

    if grid:
        far = weight_grad(3).astype(BF16)
        far_x = swap(far[:half], "dp", 1)
        far_y = swap(far[half:], "dp", 2)
        near_x = weight_grad(1)
        near_y = weight_grad(2)
        own = weight_grad(0)
        near_y = jnp.concatenate([near_y[:half] + far_x.astype(F32), near_y[half:]], axis=0)
        near_x = jnp.concatenate([near_x[:half], near_x[half:] + far_y.astype(F32)], axis=0)
        from_x = swap(near_x.astype(BF16), "dp", 1)
        from_y = swap(near_y.astype(BF16), "dp", 2)
    else:
        partial = lax.dot_general(
            tokens, spread, (((0,), (0,)), ((), ())), preferred_element_type=F32
        ).astype(BF16)

    back = []
    for r in range(owners):
        dense = jnp.dot(blocks[r], full_weight, preferred_element_type=F32).astype(BF16)
        dense = dense.reshape(tok_count, local_experts, hidden_width)
        chosen = jnp.concatenate(
            [
                jnp.dot(picks[r][e], dense[:, e], preferred_element_type=F32).astype(BF16)
                for e in range(local_experts)
            ],
            axis=0,
        )
        back.append(chosen if r == 0 else swap(chosen, "expert", r))
    back = jnp.concatenate(back, axis=0)
    grad_act = lax.dot_general(
        pick, back, (((0,), (0,)), ((), ())), preferred_element_type=F32
    )
    grad_hidden = (
        grad_act.reshape(tok_count, top_count, hidden_width)
        * gate_weight.astype(F32)[:, :, None]
    ).astype(BF16)
    grad_gate = (
        jnp.sum(grad_act * hidden.astype(F32), axis=1)
        .reshape(tok_count, top_count)
        .astype(BF16)
    )
    if grid:
        grad_down = own + from_x.astype(F32) + from_y.astype(F32)
    else:
        grad_down = lax.psum_scatter(partial, "dp", scatter_dimension=0, tiled=True).astype(F32)
    return grad_hidden, grad_gate, grad_down.reshape(rows, local_experts, hidden_width)


def solution(mesh):
    in_specs = (
        P(("dp", "expert"), None),
        P(("dp", "expert"), None, None),
        P(("dp", "expert"), None),
        P(("dp", "expert"), None),
        P("dp", "expert", None),
    )
    out_specs = (
        P(("dp", "expert"), None, None),
        P(("dp", "expert"), None),
        P("dp", "expert", None),
    )
    return jax.shard_map(
        per_device, mesh=mesh, in_specs=in_specs, out_specs=out_specs, check_vma=False
    )
```

```python
import functools

import jax
import jax.numpy as jnp
from jax import lax
from jax.experimental import pallas as pl
from jax.experimental.pallas import tpu as pltpu
from jax.sharding import PartitionSpec as P


F32 = jnp.float32
BF16 = jnp.bfloat16


def swap(value, axis, shift):
    size = lax.axis_size(axis)
    return lax.ppermute(value, axis, [(i, i ^ shift) for i in range(size)])

MESH = pl.DeviceIdType.MESH
ORDER = (3, 1, 2, 0)
ON_ROWS = (((0,), (0,)), ((), ()))


def flip(value, shift):
    out, bit = value, 1
    while bit <= shift:
        if shift & bit:
            out = out + bit - 2 * bit * lax.rem(lax.div(value, bit), 2)
        bit *= 2
    return out


def matmul(a, b):
    return jnp.dot(a, b, preferred_element_type=F32)


def fused_kernel(
    dims,
    og_ref,
    hid_ref,
    gate_ref,
    ids_ref,
    w_ref,
    gh_ref,
    gg_ref,
    down_ref,
    toks,
    wrem,
    pick,
    gated,
    packed,
    arr,
    spread,
    far,
    far_in,
    near,
    near_out,
    near_in,
    dense,
    upack,
    back,
    gate_col,
    og_send,
    og_recv,
    hs_send,
    hs_recv,
    u_send,
    u_recv,
    w_send,
    w_recv,
    g_send,
    g_recv,
):
    owners, local, cap, tok, top, ff = dims
    rows, wide = w_ref.shape
    half = rows // 2
    pair = local * cap
    slots = owners * pair
    me = lax.axis_index("expert")
    part = lax.axis_index("dp")

    barrier = pltpu.get_barrier_semaphore()
    for r in range(1, owners):
        pl.semaphore_signal(
            barrier, inc=1, device_id={"expert": flip(me, r)}, device_id_type=MESH
        )
    for q in (1, 2):
        pl.semaphore_signal(barrier, inc=1, device_id={"dp": flip(part, q)}, device_id_type=MESH)
    pl.semaphore_wait(barrier, owners + 1)

    def remote(source, target, send, recv, axis, shift):
        here = me if axis == "expert" else part
        return pltpu.make_async_remote_copy(
            src_ref=source,
            dst_ref=target,
            send_sem=send,
            recv_sem=recv,
            device_id={axis: flip(here, shift)},
            device_id_type=MESH,
        )

    low, high = pl.ds(0, half), pl.ds(half, half)
    w_moves = [
        remote(w_ref.at[high], wrem.at[0, high], w_send.at[0], w_recv.at[0], "dp", 1),
        remote(w_ref.at[low], wrem.at[1, low], w_send.at[1], w_recv.at[1], "dp", 2),
        remote(w_ref.at[low], wrem.at[0, low], w_send.at[2], w_recv.at[2], "dp", 1),
        remote(w_ref.at[high], wrem.at[1, high], w_send.at[3], w_recv.at[3], "dp", 2),
        remote(wrem.at[0, high], wrem.at[2, high], w_send.at[4], w_recv.at[4], "dp", 2),
        remote(wrem.at[1, low], wrem.at[2, low], w_send.at[5], w_recv.at[5], "dp", 1),
    ]
    for move in w_moves[:4]:
        move.start()

    def columns(q):
        return pl.ds(pl.multiple_of(flip(part, q) * rows, rows), rows)

    og_moves = {}
    for q in ORDER:
        for r in range(1, owners):
            if r == 6:
                source, shift = toks.at[q, 4], 2
            elif r == 1 or r % 2 == 0:
                source, shift = og_ref.at[:, columns(q)], r
            else:
                source, shift = toks.at[q, r - 1], 1
            og_moves[q, r] = remote(
                source, toks.at[q, r], og_send.at[q, r], og_recv.at[q, r], "expert", shift
            )

    def send_tokens(q):
        for r in (1, 4, 2):
            og_moves[q, r].start()
        toks[q, 0] = og_ref[:, columns(q)]

    def pass_tokens(q):
        og_moves[q, 4].wait_recv()
        og_moves[q, 6].start()
        og_moves[q, 5].start()
        og_moves[q, 2].wait_recv()
        og_moves[q, 3].start()

    def have_tokens(q):
        og_moves[q, 6].wait_recv()
        og_moves[q, 7].start()
        for r in (1,) + tuple(range(3, owners, 2)):
            og_moves[q, r].wait_recv()

    send_tokens(ORDER[0])

    lanes = lax.broadcasted_iota(jnp.int32, (tok, tok), 1)
    subs = lax.broadcasted_iota(jnp.int32, (tok, tok), 0)
    below = jnp.where(subs > lanes, 1.0, 0.0).astype(BF16)
    unit = jnp.where(subs == lanes, 1.0, 0.0).astype(BF16)
    both = jnp.concatenate([ids_ref[...].astype(F32), gate_ref[...].astype(F32)], axis=0)
    upright = lax.dot_general(
        both.astype(BF16), unit[: 2 * top], ON_ROWS, preferred_element_type=F32
    )
    ids = upright[:, :top].astype(jnp.int32)
    rel = flip_value(lax.div(ids, local), me, owners) * local + lax.rem(ids, local)
    named = jnp.zeros((tok, tok), F32)
    for k in range(top):
        named = jnp.where(rel[:, k : k + 1] == lanes, 1.0, named)
    position = matmul(below, named.astype(BF16))
    key = jnp.where(named > 0.5, position, -1.0).astype(BF16)
    key_t = lax.dot_general(key, unit, ON_ROWS, preferred_element_type=F32)
    for r in range(owners):
        packed[r, pl.ds(pair, 16), :] = jnp.zeros((16, ff), BF16)
        packed[r, pl.ds(pair, 16), pl.ds(0, tok)] = key_t[r * local : r * local + 16].astype(BF16)
    table = jnp.zeros((tok, tok), F32)
    for k in range(top):
        number = rel[:, k : k + 1]
        place = jnp.sum(jnp.where(number == lanes, position, 0.0), axis=1, keepdims=True)
        table = jnp.where(lanes == k, number.astype(F32), table)
        table = jnp.where(lanes == top + k, place, table)
        table = jnp.where(lanes == 2 * top + k, upright[:, top + k : top + k + 1], table)
    table = table.astype(BF16)
    slot_lanes = lax.broadcasted_iota(jnp.int32, (tok, slots), 1)
    turn = lax.rem(subs, top)
    for c in range(top):
        span = pl.ds(c * tok, tok)
        start = (lanes - c * (tok // top)) * top
        spot = jnp.where((subs >= start) & (subs < start + top), 1.0, 0.0).astype(BF16)
        shown = matmul(spot, table)

        def pull(offset):
            return jnp.sum(jnp.where(lanes == turn + offset, shown, 0.0), axis=1, keepdims=True)

        slot = (pull(0) * cap + pull(top)).astype(jnp.int32)
        pick[span, :] = jnp.where(slot == slot_lanes, 1.0, 0.0).astype(BF16)
        gates = pull(2 * top)
        gate_col[span, :] = jnp.broadcast_to(gates, (tok, tok))
        gated[span, :] = (hid_ref[span, :].astype(F32) * gates).astype(BF16)
    for c in range(owners // 2):
        two = lax.dot_general(
            pick[:, pl.ds(c * 2 * pair, 2 * pair)],
            gated[...],
            ON_ROWS,
            preferred_element_type=F32,
        ).astype(BF16)
        packed[2 * c, pl.ds(0, pair), :] = two[:pair]
        packed[2 * c + 1, pl.ds(0, pair), :] = two[pair:]

    hs_moves = [None] + [
        remote(packed.at[r], arr.at[r], hs_send.at[r], hs_recv.at[r], "expert", r)
        for r in range(1, owners)
    ]
    for r in range(owners - 1, 0, -1):
        hs_moves[r].start()
    for q in ORDER[1:]:
        send_tokens(q)
    arr[0] = packed[0]

    pass_tokens(ORDER[0])
    w_moves[0].wait_recv()
    w_moves[4].start()
    w_moves[1].wait_recv()
    w_moves[5].start()

    places = lax.broadcasted_iota(jnp.int32, (cap, tok), 0).astype(F32)

    def chosen(r, e):
        row = arr[r, pl.ds(pair, 16), pl.ds(0, tok)].astype(F32)[e : e + 1]
        return jnp.where(row == places, 1.0, 0.0).astype(BF16)

    for r in range(owners):
        if r:
            hs_moves[r].wait_recv()
        for e in range(local):
            spread[pl.ds(r * tok, tok), pl.ds(e * ff, ff)] = lax.dot_general(
                chosen(r, e),
                arr[r, pl.ds(e * cap, cap), :],
                ON_ROWS,
                preferred_element_type=F32,
            ).astype(BF16)

    def weight_grad(q, store):
        @pl.loop(0, local)
        def _(e):
            at = pl.ds(pl.multiple_of(e * ff, ff), ff)
            store(
                at,
                lax.dot_general(
                    toks[q].reshape(owners * tok, rows),
                    spread[:, at],
                    ON_ROWS,
                    preferred_element_type=F32,
                ),
            )

    def keep_far(at, value):
        far[:, at] = value.astype(BF16)

    have_tokens(3)
    weight_grad(3, keep_far)
    far_moves = [
        remote(far.at[low], far_in.at[0], g_send.at[0], g_recv.at[0], "dp", 1),
        remote(far.at[high], far_in.at[1], g_send.at[1], g_recv.at[1], "dp", 2),
    ]
    for move in far_moves:
        move.start()
    first = {1: low, 2: high}
    last = {1: high, 2: low}
    near_moves = {}
    for q in (1, 2):
        for n, span in enumerate((first[q], last[q])):
            i = 2 * q + n
            near_moves[q, n] = remote(
                near_out.at[q - 1, span],
                near_in.at[q - 1, span],
                g_send.at[i],
                g_recv.at[i],
                "dp",
                q,
            )
    pass_tokens(1)
    for q in (1, 2):
        have_tokens(q)
        pass_tokens((0, 2, 0)[q])

        def keep_near(at, value):
            near[q - 1, :, at] = value[half:] if q == 1 else value[:half]
            free = value[:half] if q == 1 else value[half:]
            near_out[q - 1, first[q], at] = free.astype(BF16)

        weight_grad(q, keep_near)
        near_moves[q, 0].start()
    have_tokens(0)

    def close(q):
        far_moves[2 - q].wait_recv()
        near_out[q - 1, last[q], :] = (near[q - 1] + far_in[2 - q].astype(F32)).astype(BF16)
        near_moves[q, 1].start()

    for i in (2, 3, 4, 5):
        w_moves[i].wait_recv()

    u_moves = [None] + [
        remote(upack.at[r], back.at[r], u_send.at[r], u_recv.at[r], "expert", r)
        for r in range(1, owners)
    ]
    group_size = owners // 2
    for g in (1, 0):
        span = pl.ds(g * group_size, group_size)

        @pl.loop(0, local)
        def _(e):
            at = pl.ds(pl.multiple_of(e * ff, ff), ff)
            total = matmul(toks[0, span].reshape(group_size * tok, rows), w_ref[:, at])
            for q in (1, 2, 3):
                total += matmul(
                    toks[q, span].reshape(group_size * tok, rows), wrem[q - 1, :, at]
                )
            dense[:, at] = total.astype(BF16)

        for i in range(group_size - 1, -1, -1):
            r = g * group_size + i
            for e in range(local):
                value = matmul(
                    chosen(r, e), dense[pl.ds(i * tok, tok), pl.ds(e * ff, ff)]
                ).astype(BF16)
                if r:
                    upack[r, pl.ds(e * cap, cap), :] = value
                else:
                    back[0, pl.ds(e * cap, cap), :] = value
            if r:
                u_moves[r].start()
        if g:
            close(2)
            close(1)

    def keep_own(at, value):
        down_ref[:, at] = value

    weight_grad(0, keep_own)

    for r in range(1, owners):
        u_moves[r].wait_recv()
    every = back[...].reshape(slots, ff)
    totals = []
    for c in range(0, top, 2):
        acts = matmul(pick[pl.ds(c * tok, 2 * tok), :], every)
        for j in range(2):
            span = pl.ds((c + j) * tok, tok)
            act = acts[j * tok : (j + 1) * tok]
            gh_ref[span, :] = (act * gate_col[span, 0:1]).astype(BF16)
            dot = jnp.sum(act * hid_ref[span, :].astype(F32), axis=1, keepdims=True)
            dot = jnp.where(lanes == turn, dot, 0.0)
            totals.append(jnp.sum(dot.reshape(tok // top, top, tok), axis=1))
    gg_ref[...] = jnp.transpose(jnp.concatenate(totals, axis=0))[:top]

    for q in (1, 2):
        for n in (0, 1):
            near_moves[q, n].wait_recv()
    down_ref[...] += near_in[0].astype(F32) + near_in[1].astype(F32)

    for move in w_moves + far_moves + hs_moves[1:] + u_moves[1:]:
        move.wait_send()
    for move in list(near_moves.values()) + list(og_moves.values()):
        move.wait_send()


def flip_value(group, me, owners):
    out, bit = group, 1
    while bit < owners:
        mine = lax.rem(lax.div(me, bit), 2)
        theirs = lax.rem(lax.div(group, bit), 2)
        out = out + bit * mine * (1 - 2 * theirs)
        bit *= 2
    return out


def fused(out_grad, saved_hidden, gate_weight, expert_ids, down_weight):
    tok, width = out_grad.shape
    top, ff = saved_hidden.shape[1:]
    owners = lax.axis_size("expert")
    rows, local = down_weight.shape[:2]
    wide = local * ff
    cap = max(2, 3 * tok * top // (2 * local * owners))
    pair = local * cap
    half = rows // 2
    dims = (owners, local, cap, tok, top, ff)
    vmem = pl.BlockSpec(memory_space=pltpu.VMEM)
    dma = pltpu.SemaphoreType.DMA
    grad_act, totals, grad_down = pl.pallas_call(
        functools.partial(fused_kernel, dims),
        out_shape=(
            jax.ShapeDtypeStruct((top * tok, ff), BF16),
            jax.ShapeDtypeStruct((top, tok), F32),
            jax.ShapeDtypeStruct((rows, wide), F32),
        ),
        in_specs=[vmem] * 5,
        out_specs=(vmem,) * 3,
        scratch_shapes=[
            pltpu.VMEM((4, owners, tok, rows), BF16),
            pltpu.VMEM((3, rows, wide), BF16),
            pltpu.VMEM((top * tok, owners * pair), BF16),
            pltpu.VMEM((top * tok, ff), BF16),
            pltpu.VMEM((owners, pair + 16, ff), BF16),
            pltpu.VMEM((owners, pair + 16, ff), BF16),
            pltpu.VMEM((owners * tok, wide), BF16),
            pltpu.VMEM((rows, wide), BF16),
            pltpu.VMEM((2, half, wide), BF16),
            pltpu.VMEM((2, half, wide), F32),
            pltpu.VMEM((2, rows, wide), BF16),
            pltpu.VMEM((2, rows, wide), BF16),
            pltpu.VMEM((owners // 2 * tok, wide), BF16),
            pltpu.VMEM((owners, pair, ff), BF16),
            pltpu.VMEM((owners, pair, ff), BF16),
            pltpu.VMEM((top * tok, tok), F32),
            dma((4, owners)),
            dma((4, owners)),
            dma((owners,)),
            dma((owners,)),
            dma((owners,)),
            dma((owners,)),
            dma((6,)),
            dma((6,)),
            dma((6,)),
            dma((6,)),
        ],
        compiler_params=pltpu.CompilerParams(
            collective_id=0, has_side_effects=True, vmem_limit_bytes=62 << 20
        ),
    )(
        out_grad,
        saved_hidden.reshape(tok * top, ff),
        gate_weight.T,
        expert_ids.T,
        down_weight.reshape(rows, wide),
    )
    return (
        grad_act.reshape(tok, top, ff),
        totals.T.astype(BF16),
        grad_down.reshape(rows, local, ff),
    )


def per_device(out_grad, saved_hidden, gate_weight, expert_ids, down_weight):
    if lax.axis_size("dp") == 4 and lax.axis_size("expert") == 8:
        return fused(out_grad, saved_hidden, gate_weight, expert_ids, down_weight)
    tok_count, width = out_grad.shape
    top_count = expert_ids.shape[1]
    hidden_width = saved_hidden.shape[2]
    owners = lax.axis_size("expert")
    parts = lax.axis_size("dp")
    rows = width // parts
    local_experts = down_weight.shape[1]
    total_experts = local_experts * owners
    capacity = max(2, 3 * tok_count * top_count // (2 * total_experts))
    route_count = tok_count * top_count
    pair_slots = local_experts * capacity
    slot_count = owners * pair_slots
    wide = local_experts * hidden_width
    me = lax.axis_index("expert")
    my_part = lax.axis_index("dp")
    grid = parts == 4

    if grid:
        og = jnp.concatenate(
            [
                lax.dynamic_slice_in_dim(out_grad, (my_part ^ q) * rows, rows, axis=1)
                for q in range(parts)
            ],
            axis=1,
        )
    else:
        og = out_grad
    weight = down_weight.reshape(rows, wide)

    blocks = [None] * owners
    blocks[0] = og
    for r in range(2, owners, 2):
        blocks[r] = swap(og, "expert", r)
    if grid:
        wx = swap(weight, "dp", 1)
        wy = swap(weight, "dp", 2)

    rel = ((expert_ids // local_experts) ^ me) * local_experts + expert_ids % local_experts
    one_hot = rel[:, :, None] == jnp.arange(total_experts, dtype=jnp.int32)
    named = jnp.any(one_hot, axis=1)
    below = (
        jnp.arange(tok_count)[:, None] > jnp.arange(tok_count)[None, :]
    ).astype(BF16)
    position = jnp.dot(below, named.astype(BF16), preferred_element_type=F32)
    key = jnp.where(named, position, -1.0).astype(BF16)
    route_pos = jnp.sum(jnp.where(one_hot, position[:, None, :], 0.0), axis=2)
    slot = (rel * capacity + route_pos.astype(jnp.int32)).reshape(route_count)
    pick = (jnp.arange(slot_count, dtype=jnp.int32)[:, None] == slot[None, :]).astype(BF16)
    hidden = saved_hidden.reshape(route_count, hidden_width)
    gated = (saved_hidden.astype(F32) * gate_weight.astype(F32)[:, :, None]).astype(BF16)
    packed = jnp.dot(
        pick, gated.reshape(route_count, hidden_width), preferred_element_type=F32
    ).astype(BF16)
    key_rows = jnp.pad(
        key.T.reshape(owners, local_experts, tok_count),
        ((0, 0), (0, 16 - local_experts), (0, hidden_width - tok_count)),
    )
    packed = jnp.concatenate(
        [packed.reshape(owners, pair_slots, hidden_width), key_rows], axis=1
    )
    arrived = [packed[0]] + [swap(packed[r], "expert", r) for r in range(1, owners)]
    for r in range(0, owners, 2):
        blocks[r + 1] = swap(blocks[r], "expert", 1)
    if grid:
        half = rows // 2
        wd = jnp.concatenate(
            [swap(wy[:half], "dp", 1), swap(wx[half:], "dp", 2)], axis=0
        )
        full_weight = jnp.concatenate([weight, wx, wy, wd], axis=0)
    else:
        full_weight = lax.all_gather(weight, "dp", axis=0, tiled=True)

    places = jnp.arange(capacity, dtype=jnp.int32).astype(BF16)
    picks, spread = [], []
    for r in range(owners):
        key_in = arrived[r][pair_slots : pair_slots + local_experts, :tok_count]
        chosen = (key_in[:, None, :] == places[None, :, None]).astype(BF16)
        picks.append(chosen)
        slots_in = arrived[r][:pair_slots].reshape(local_experts, capacity, hidden_width)
        spread.append(
            jnp.concatenate(
                [
                    jnp.dot(chosen[e].T, slots_in[e], preferred_element_type=F32).astype(BF16)
                    for e in range(local_experts)
                ],
                axis=1,
            )
        )
    spread = jnp.concatenate(spread, axis=0)
    tokens = jnp.concatenate(blocks, axis=0)

    def weight_grad(q):
        return lax.dot_general(
            tokens[:, q * rows : (q + 1) * rows],
            spread,
            (((0,), (0,)), ((), ())),
            preferred_element_type=F32,
        )

    if grid:
        far = weight_grad(3).astype(BF16)
        far_x = swap(far[:half], "dp", 1)
        far_y = swap(far[half:], "dp", 2)
        near_x = weight_grad(1)
        near_y = weight_grad(2)
        own = weight_grad(0)
        near_y = jnp.concatenate([near_y[:half] + far_x.astype(F32), near_y[half:]], axis=0)
        near_x = jnp.concatenate([near_x[:half], near_x[half:] + far_y.astype(F32)], axis=0)
        from_x = swap(near_x.astype(BF16), "dp", 1)
        from_y = swap(near_y.astype(BF16), "dp", 2)
    else:
        partial = lax.dot_general(
            tokens, spread, (((0,), (0,)), ((), ())), preferred_element_type=F32
        ).astype(BF16)

    back = []
    for r in range(owners):
        dense = jnp.dot(blocks[r], full_weight, preferred_element_type=F32).astype(BF16)
        dense = dense.reshape(tok_count, local_experts, hidden_width)
        chosen = jnp.concatenate(
            [
                jnp.dot(picks[r][e], dense[:, e], preferred_element_type=F32).astype(BF16)
                for e in range(local_experts)
            ],
            axis=0,
        )
        back.append(chosen if r == 0 else swap(chosen, "expert", r))
    back = jnp.concatenate(back, axis=0)
    grad_act = lax.dot_general(
        pick, back, (((0,), (0,)), ((), ())), preferred_element_type=F32
    )
    grad_hidden = (
        grad_act.reshape(tok_count, top_count, hidden_width)
        * gate_weight.astype(F32)[:, :, None]
    ).astype(BF16)
    grad_gate = (
        jnp.sum(grad_act * hidden.astype(F32), axis=1)
        .reshape(tok_count, top_count)
        .astype(BF16)
    )
    if grid:
        grad_down = own + from_x.astype(F32) + from_y.astype(F32)
    else:
        grad_down = lax.psum_scatter(partial, "dp", scatter_dimension=0, tiled=True).astype(F32)
    return grad_hidden, grad_gate, grad_down.reshape(rows, local_experts, hidden_width)


def solution(mesh):
    in_specs = (
        P(("dp", "expert"), None),
        P(("dp", "expert"), None, None),
        P(("dp", "expert"), None),
        P(("dp", "expert"), None),
        P("dp", "expert", None),
    )
    out_specs = (
        P(("dp", "expert"), None, None),
        P(("dp", "expert"), None),
        P("dp", "expert", None),
    )
    return jax.shard_map(
        per_device, mesh=mesh, in_specs=in_specs, out_specs=out_specs, check_vma=False
    )
```
